256 devices in a mesh: vertex: 64 (over x, y_lo, z), feat: 4 (over y_hi, core).
Axes of the slice: x: 4, y: 4 (y_hi: 2, y_lo: 2; y = y_hi * 2 + y_lo), z: 8, core: 2. Of those that a mesh axis runs over, the one named last changes fastest.
Arguments:
- features: bfloat16 [196608, 512], P('vertex', 'feat'), may hold values from -6 to 6
- tiles: bfloat16 [24576, 128, 128], P('vertex'), as said below
- tile_row: int32 [24576], P('vertex'), may hold values from 0 to 24, as said below
- tile_col: int32 [24576], P('vertex'), may hold values from 0 to 1535, as said below
- permutation: int32 [196608], P('vertex'), may hold values from 0 to 196607, as said below
- weight: bfloat16 [512, 512], P('feat'), may hold values from -0.25 to 0.25
- cotangent: bfloat16 [196608, 512], P('vertex', 'feat'), may hold values from -6 to 6
Outputs:
- activations: bfloat16 [196608, 512], P('vertex', 'feat')
- grad_features: bfloat16 [196608, 512], P('vertex', 'feat')
- grad_weight: float32 [512, 512], P('feat')
The draws below stay inside these ranges and needn't reach their ends.
Inputs may be any that keep to these rules, and one draw needn't show every extreme that they name: `tile_row`: the live slots of a device come first; a slot with row 24 is empty and its tile is zero; some device has all 384 slots live in every draw. `tile_col`: every tile's column block lies on a device at most 3 positions away from the tile's own device around the vertex axis, wrapping at its ends; an empty slot names its device's first block. Empty slots hold zero tiles. Each device's 24 * 128 consecutive entries are a permutation of that device's own node numbers.
All inputs are finite; a program needn't handle non-finite values.
Results may differ from the reference program's by a relative error of at most 0.0061.
Values may be sent and summed in bfloat16 or wider, within the bound.
No kernel may reach another device: no remote copies, remote signals or barrier semaphores. Data moves between devices by JAX's collectives and lax.ppermute only.
A program may use at most 128 MiB of HBM per device.

```python
import math
import jax
import jax.numpy as jnp
from jax import lax

D = 512
SIDE = 128
RB_DEV = 24
TILE_CAP = 384
REACH = 3
NODES = 196608
TILES = 24576
N_VERTEX = 64


def layout(key):
    base = jax.random.fold_in(key, 7)
    key_a, key_b, key_c, key_d, key_e = jax.random.split(base, 5)
    counts = jax.random.randint(key_a, (N_VERTEX,), TILE_CAP // 4, TILE_CAP // 2 + 1)
    filled = jax.random.randint(key_b, (), 0, N_VERTEX)
    counts = jnp.where(jnp.arange(N_VERTEX) == filled, TILE_CAP, counts)
    slot = jnp.arange(TILE_CAP)[None, :]
    device = jnp.arange(N_VERTEX)[:, None]
    live = slot < counts[:, None]
    diagonal = slot < RB_DEV
    rand_row = jax.random.randint(key_c, (N_VERTEX, TILE_CAP), 0, RB_DEV)
    offset = jax.random.randint(key_d, (N_VERTEX, TILE_CAP), -REACH, REACH + 1)
    local_col = jax.random.randint(key_e, (N_VERTEX, TILE_CAP), 0, RB_DEV)
    row = jnp.where(diagonal, slot, rand_row)
    row = jnp.where(live, row, RB_DEV)
    owner = (device + jnp.where(diagonal, 0, offset) + N_VERTEX) % N_VERTEX
    col = owner * RB_DEV + jnp.where(diagonal, slot, local_col)
    col = jnp.where(live, col, device * RB_DEV)
    return (row.reshape(-1).astype(jnp.int32), col.reshape(-1).astype(jnp.int32), live.reshape(-1))


def draw_tile_row(key, part):
    row, col, live = layout(key)
    return row


def draw_tile_col(key, part):
    row, col, live = layout(key)
    return col


def draw_tiles(key, part):
    row, col, live = layout(key)
    noise = jax.random.fold_in(key, 11)
    key_a, key_b = jax.random.split(noise)
    present = jax.random.uniform(key_a, (TILES, SIDE, SIDE)) < 0.4
    values = jnp.exp(jax.random.uniform(key_b, (TILES, SIDE, SIDE), minval=-0.7, maxval=0.7))
    scale = (0.45 * SIDE * 4.0) ** (-0.5)
    result = jnp.where(present, values, 0.0) * scale * live.astype(jnp.float32)[:, None, None]
    return result.astype(jnp.float32).astype(jnp.bfloat16)


def draw_permutation(key, part):
    base = jax.random.fold_in(key, 23)
    rows = RB_DEV * SIDE
    keys = jax.random.split(base, N_VERTEX)
    local = jax.vmap(lambda one: jax.random.permutation(one, rows))(keys)
    return (local + jnp.arange(N_VERTEX)[:, None] * rows).reshape(-1).astype(jnp.int32)


def block_scale(rng, extent, cuts, smallest, high):
    def one(position, blocks):
        steps = jax.random.uniform(jax.random.fold_in(jax.random.fold_in(rng, 6), position), (blocks,), jnp.float32, smallest / len(cuts), high / len(cuts))
        return jnp.repeat(jnp.exp(steps), extent[position] // blocks).reshape((-1,) + (1,) * (len(extent) - position - 1))

    factor_of = one(*cuts[0])
    for cut in cuts[1:]:
        factor_of = factor_of * one(*cut)
    return factor_of


def scatter_about(key, extent, width, most, shards=(), kind=jnp.bfloat16):
    gain = block_scale(key, extent, shards, -0.22, 0.18) if shards else 1.0
    values = jax.random.normal(key, extent, jnp.float32) * width * gain
    return jnp.minimum(jnp.maximum(values, -most), most).astype(kind)


def setup_inputs(seed: int = 0) -> dict:
    seeds = jax.random.split(jax.random.key(seed), 8)
    return {
        "features": scatter_about(seeds[0], (NODES, D), 1.0, 6.0, ((0, 64), (1, 4))),
        "tiles": draw_tiles(jax.random.fold_in(seeds[7], 71), 0),
        "tile_row": draw_tile_row(jax.random.fold_in(seeds[7], 71), 0),
        "tile_col": draw_tile_col(jax.random.fold_in(seeds[7], 71), 0),
        "permutation": draw_permutation(jax.random.fold_in(seeds[7], 71), 0),
        "weight": scatter_about(seeds[5], (D, D), D ** -0.5, 0.25, ((0, 4),)),
        "cotangent": scatter_about(seeds[6], (NODES, D), 1.0, 6.0, ((0, 64), (1, 4))),
    }


def reference(features, tiles, tile_row, tile_col, permutation, weight, cotangent):
    ordered = jnp.take(features, permutation, axis=0)
    blocked = ordered.reshape(RB_DEV * N_VERTEX, SIDE, D)
    tile_groups = tiles.reshape(N_VERTEX, TILE_CAP, SIDE, SIDE)
    row_groups = tile_row.reshape(N_VERTEX, TILE_CAP)
    col_groups = tile_col.reshape(N_VERTEX, TILE_CAP)
    block_ids = jnp.arange(RB_DEV, dtype=jnp.int32)

    def forward_device(carry, inputs):
        tile_g, row_g, col_g = inputs
        gathered = jnp.take(blocked, col_g, axis=0).astype(jnp.float32)
        product = jnp.einsum('tij,tjf->tif', tile_g.astype(jnp.float32), gathered, precision=lax.Precision.HIGHEST)
        onehot = (row_g[None, :] == block_ids[:, None]).astype(jnp.float32)
        return (carry, jnp.einsum('rt,tif->rif', onehot, product, precision=lax.Precision.HIGHEST))
    _, parts = lax.scan(forward_device, jnp.float32(0.0), (tile_groups, row_groups, col_groups))
    aggregated = parts.reshape(NODES, D).astype(jnp.bfloat16)
    mixed = jnp.dot(aggregated, weight, preferred_element_type=jnp.float32)
    activations = jax.nn.silu(mixed).astype(jnp.bfloat16)
    sig = jax.nn.sigmoid(mixed)
    grad_mixed = (cotangent.astype(jnp.float32) * sig * (1.0 + mixed * (1.0 - sig))).astype(jnp.bfloat16)
    grad_weight = jnp.dot(aggregated.T, grad_mixed, preferred_element_type=jnp.float32) * (1.0 / math.sqrt(NODES))
    grad_aggregated = jnp.dot(grad_mixed, weight.T, preferred_element_type=jnp.float32).astype(jnp.bfloat16)
    grad_blocks = grad_aggregated.reshape(RB_DEV * N_VERTEX, SIDE, D)
    device_ids = jnp.arange(N_VERTEX, dtype=jnp.int32)

    def backward_device(total, inputs):
        tile_g, row_g, col_g, device = inputs
        global_row = device * RB_DEV + jnp.minimum(row_g, RB_DEV - 1)
        source = jnp.take(grad_blocks, global_row, axis=0).astype(jnp.float32)
        contrib = jnp.einsum('tji,tjf->tif', tile_g.astype(jnp.float32), source, precision=lax.Precision.HIGHEST)
        return (total.at[col_g].add(contrib), None)
    start = jnp.zeros((RB_DEV * N_VERTEX, SIDE, D), jnp.float32)
    total, _ = lax.scan(backward_device, start, (tile_groups, row_groups, col_groups, device_ids))
    grad_ordered = total.reshape(NODES, D).astype(jnp.bfloat16)
    grad_features = jnp.zeros((NODES, D), jnp.bfloat16).at[permutation].set(grad_ordered)
    return (activations, grad_features, grad_weight)
```

```python
import functools
import math

import jax
import jax.numpy as jnp
from jax import lax
from jax.experimental import pallas as pl
from jax.experimental.pallas import tpu as pltpu
from jax.sharding import PartitionSpec as P

REACH = 3
PARTS = 2
GROUPS = (2 * REACH + 1) * PARTS
unroll = 4
ring = 16
row_bits = 5
col_bits = 5

f32 = jnp.float32
bf16 = jnp.bfloat16
SMEM = pl.BlockSpec(memory_space=pltpu.SMEM)
VMEM = pl.BlockSpec(memory_space=pltpu.VMEM)
HBM = pl.BlockSpec(memory_space=pltpu.HBM)


def shift(value, steps):
    count = lax.axis_size("vertex")
    pairs = [(source, (source + steps) % count) for source in range(count)]
    return lax.ppermute(value, "vertex", pairs)


def slot_plan(tile_row, tile_col, here, blocks, devices):
    slots = tile_row.shape[0]
    owner = tile_col // blocks
    local = tile_col - owner * blocks
    span = blocks // PARTS
    part = local // span
    group = (owner - here + REACH + devices) % devices * PARTS + part
    group = jnp.where(tile_row < blocks, group, GROUPS)
    slot = jnp.arange(slots, dtype=jnp.int32)
    packed = (slot << (row_bits + col_bits)) | (tile_row << col_bits) | (local - part * span)
    same = (group[:, None] == group[None, :]) & (slot[None, :] < slot[:, None])
    rank = jnp.sum(same.astype(jnp.int32), axis=1)
    ids = jnp.arange(GROUPS, dtype=jnp.int32)
    counts = jnp.sum((group[:, None] == ids[None, :]).astype(jnp.int32), axis=0)
    steps = (counts + unroll - 1) // unroll
    ends = jnp.sum(jnp.where(ids[:, None] >= ids[None, :], steps[None, :], 0), axis=1)
    starts = ends - steps
    base = jnp.sum(jnp.where(group[:, None] == ids[None, :], starts[None, :], 0), axis=1)
    place = jnp.where(group < GROUPS, base * unroll + rank, -1)
    places = slots + GROUPS * unroll
    dummy = blocks << col_bits
    index = jnp.arange(places, dtype=jnp.int32)
    plan = dummy + jnp.sum(
        jnp.where(index[:, None] == place[None, :], packed[None, :] - dummy, 0), axis=1
    )
    return plan, jnp.concatenate([starts, ends])


def gather_kernel(perm, base, source, out, wide, moved):
    rows = out.shape[0]
    wide[...] = source[...].astype(f32)
    first = base[0]

    @pl.loop(0, rows // 16)
    def _(step):
        at = step * 16
        for j in range(16):
            moved[pl.ds(at + j, 1), :] = wide[pl.ds(perm[at + j] - first, 1), :]

    out[...] = moved[...].astype(out.dtype)


def gather_rows(perm, base, source):
    shape = (perm.shape[0], source.shape[1])
    return pl.pallas_call(
        gather_kernel,
        out_shape=jax.ShapeDtypeStruct(shape, source.dtype),
        in_specs=[SMEM, SMEM, VMEM],
        out_specs=VMEM,
        scratch_shapes=[pltpu.VMEM(source.shape, f32), pltpu.VMEM(shape, f32)],
        cost_estimate=pl.CostEstimate(flops=0, bytes_accessed=4 * source.size, transcendentals=0),
        name="gather_rows",
    )(perm, base, source)


def each_slot(plan, tiles, buffer, sems, start, end, use):
    total = (end - start) * unroll
    first = start * unroll

    def copy(k):
        slot = plan[first + k] >> (row_bits + col_bits)
        at = lax.rem(k, ring)
        return pltpu.make_async_copy(tiles.at[slot], buffer.at[at], sems.at[at])

    def prime(k, carry):
        copy(k).start()
        return carry

    lax.fori_loop(0, jnp.minimum(total, ring), prime, 0)

    def step(i, carry):
        at = i * unroll
        for j in range(unroll):
            copy(at + j).wait()
        for j in range(unroll):
            use(plan[first + at + j], buffer[lax.rem(at + j, ring)])
        for j in range(unroll):

            @pl.when(at + j + ring < total)
            def _():
                copy(at + j + ring).start()

        return carry

    lax.fori_loop(0, end - start, step, 0)


def forward_kernel(groups, first, last, plan, spans, tiles, *refs):
    windows = refs[: len(groups)]
    rest = refs[len(groups) :]
    if not first:
        total_in, rest = rest[0], rest[1:]
    out, total, buffer, sems = rest
    side = buffer.shape[-1]
    blocks = total.shape[0] - 1
    if first:
        total[...] = jnp.zeros_like(total)
    else:
        total[:blocks] = total_in[...]
    for group, window in zip(groups, windows):

        def use(packed, tile, window=window):
            row = (packed >> col_bits) & ((1 << row_bits) - 1)
            col = packed & ((1 << col_bits) - 1)
            source = window[pl.ds(pl.multiple_of(col * side, side), side), :]
            total[row] += jnp.dot(tile, source, preferred_element_type=f32)

        each_slot(plan, tiles, buffer, sems, spans[group], spans[GROUPS + group], use)
    out[...] = total[:blocks].astype(out.dtype)


def forward_group(groups, first, last, plan, spans, tiles, windows, total):
    side = tiles.shape[-1]
    blocks = PARTS * windows[0].shape[0] // side
    shape = (blocks, side, windows[0].shape[1])
    return pl.pallas_call(
        functools.partial(forward_kernel, groups, first, last),
        out_shape=jax.ShapeDtypeStruct(shape, bf16 if last else f32),
        in_specs=[SMEM, SMEM, HBM] + [VMEM] * (len(groups) + (not first)),
        out_specs=VMEM,
        scratch_shapes=[
            pltpu.VMEM((blocks + 1, *shape[1:]), f32),
            pltpu.VMEM((ring, side, side), bf16),
            pltpu.SemaphoreType.DMA((ring,)),
        ],
        cost_estimate=pl.CostEstimate(
            flops=len(groups) * 30 * 2**22, bytes_accessed=len(groups) * 30 * 2**15, transcendentals=0
        ),
        compiler_params=pltpu.CompilerParams(vmem_limit_bytes=32 * 2**20),
        name="forward_group",
    )(plan, spans, tiles, *windows, *([] if first else [total]))


def backward_kernel(groups, plan, spans, tiles, grad, *refs):
    outs = refs[: len(groups)]
    total, buffer, sems = refs[len(groups) :]
    for group, out in zip(groups, outs):
        total[...] = jnp.zeros_like(total)

        def use(packed, tile):
            row = (packed >> col_bits) & ((1 << row_bits) - 1)
            col = packed & ((1 << col_bits) - 1)
            value = jnp.dot(grad[jnp.minimum(row, grad.shape[0] - 1)], tile, preferred_element_type=f32)
            dummy = row == grad.shape[0]
            total[jnp.where(dummy, total.shape[0] - 1, col)] += value

        each_slot(plan, tiles, buffer, sems, spans[group], spans[GROUPS + group], use)
        out[...] = total[: out.shape[0]].astype(out.dtype)


def backward_group(groups, plan, spans, tiles, grad, dtype):
    blocks, width, side = grad.shape
    return pl.pallas_call(
        functools.partial(backward_kernel, groups),
        out_shape=[jax.ShapeDtypeStruct((blocks // PARTS, width, side), dtype)] * len(groups),
        in_specs=[SMEM, SMEM, HBM, VMEM],
        out_specs=[VMEM] * len(groups),
        scratch_shapes=[
            pltpu.VMEM((blocks // PARTS + 1, width, side), f32),
            pltpu.VMEM((ring, side, side), bf16),
            pltpu.SemaphoreType.DMA((ring,)),
        ],
        cost_estimate=pl.CostEstimate(
            flops=len(groups) * 30 * 2**22, bytes_accessed=len(groups) * 30 * 2**15, transcendentals=0
        ),
        compiler_params=pltpu.CompilerParams(vmem_limit_bytes=32 * 2**20),
        name="backward_group",
    )(plan, spans, tiles, grad)


def exchange(value, step):
    count = lax.axis_size("feat")
    return lax.ppermute(value, "feat", [(source, source ^ step) for source in range(count)])


def gather_feat(value):
    far = exchange(value, 2)
    return [value, exchange(value, 1), far, exchange(far, 1)]


def mix_kernel(shard, *refs):
    agg, cot, weight = refs[0:4], refs[4:8], refs[8:12]
    act, grad_agg, grad_weight = refs[-3:]
    width = agg[0].shape[1]
    columns = [pl.ds(pl.multiple_of((shard[0] ^ k) * width, width), width) for k in range(4)]
    near = jnp.concatenate([weight[0][:, c] for c in columns], axis=1)
    full = jnp.concatenate([near] + [jnp.concatenate([weight[i][:, c] for c in columns], axis=1) for i in range(1, 4)], axis=0)
    mixed = jnp.dot(jnp.concatenate([a[...] for a in agg], axis=1), full, preferred_element_type=f32)
    sig = 1.0 / (1.0 + jnp.exp(-mixed))
    cotangent = jnp.concatenate([c[...] for c in cot], axis=1).astype(f32)
    grad = (cotangent * sig * (1.0 + mixed * (1.0 - sig))).astype(bf16)
    act[...] = (mixed[:, :width] * sig[:, :width]).astype(bf16)
    back = lax.dot_general(near, grad, (((1,), (1,)), ((), ())), preferred_element_type=f32)
    side = grad_agg.shape[2]
    for b in range(grad_agg.shape[0]):
        grad_agg[b] = back[:, b * side : (b + 1) * side].astype(bf16)
    terms = lax.dot_general(agg[0][...], grad, (((0,), (0,)), ((), ())), preferred_element_type=f32)

    @pl.when(pl.program_id(0) == 0)
    def _():
        for k, c in enumerate(columns):
            grad_weight[:, c] = terms[:, k * width : (k + 1) * width]

    @pl.when(pl.program_id(0) > 0)
    def _():
        for k, c in enumerate(columns):
            grad_weight[:, c] += terms[:, k * width : (k + 1) * width]


def mix(shard, agg, cot, weight, side, block_rows):
    rows, width = agg[0].shape
    full = weight[0].shape[1]
    per = block_rows // side
    rowwise = pl.BlockSpec((block_rows, width), lambda i: (i, 0))
    whole = pl.BlockSpec((width, full), lambda i: (0, 0))
    return pl.pallas_call(
        mix_kernel,
        grid=(rows // block_rows,),
        out_shape=[
            jax.ShapeDtypeStruct((rows, width), bf16),
            jax.ShapeDtypeStruct((rows // side, width, side), bf16),
            jax.ShapeDtypeStruct((width, full), f32),
        ],
        in_specs=[SMEM] + [rowwise] * 8 + [whole] * 4,
        out_specs=[rowwise, pl.BlockSpec((per, width, side), lambda i: (i, 0, 0)), whole],
        cost_estimate=pl.CostEstimate(
            flops=3 * rows * full * full, bytes_accessed=8 * rows * full, transcendentals=rows * full
        ),
        compiler_params=pltpu.CompilerParams(vmem_limit_bytes=48 * 2**20),
        name="mix",
    )(shard, *agg, *cot, *weight)


def scatter_kernel(perm, base, *refs):
    out, moved, wide = refs[-3:]
    first = base[0]
    at_part = 0
    for part in range(PARTS):
        own, left, right = refs[part], refs[PARTS + part], refs[2 * PARTS + part]
        blocks, width, side = own.shape

        @pl.loop(0, blocks)
        def _(b):
            total = own[b].astype(f32) + left[b].astype(f32) + right[b].astype(f32)
            wide[...] = total.T
            at = at_part + b * side
            for j in range(side):
                moved[pl.ds(perm[at + j] - first, 1), :] = wide[j : j + 1, :]

        at_part += blocks * side
    out[...] = moved[...].astype(out.dtype)


def scatter_rows(perm, base, own, left, right):
    blocks, width, side = own[0].shape
    rows = PARTS * blocks * side
    return pl.pallas_call(
        scatter_kernel,
        out_shape=jax.ShapeDtypeStruct((rows, width), bf16),
        in_specs=[SMEM, SMEM] + [VMEM] * (3 * PARTS),
        out_specs=VMEM,
        scratch_shapes=[pltpu.VMEM((rows, width), f32), pltpu.VMEM((side, width), f32)],
        cost_estimate=pl.CostEstimate(flops=0, bytes_accessed=8 * rows * width, transcendentals=0),
        name="scatter_rows",
    )(perm, base, *own, *left, *right)


def add(carried, own):
    return (carried.astype(f32) + own.astype(f32)).astype(bf16)


def sum_over_vertex(value, ring):
    devices = lax.axis_size("vertex")
    inner = [[g + i for i in range(ring)] for g in range(0, devices, ring)]
    outer = [[g + i for g in range(0, devices, ring)] for i in range(ring)]
    for groups in (inner, outer):
        split = value.reshape(len(groups[0]), -1, value.shape[1])
        value = jnp.sum(lax.all_to_all(split, "vertex", 0, 0, axis_index_groups=groups, tiled=True), axis=0)
    for groups in (outer, inner):
        split = jnp.broadcast_to(value[None], (len(groups[0]), *value.shape))
        value = lax.all_to_all(split, "vertex", 0, 0, axis_index_groups=groups, tiled=True)
        value = value.reshape(-1, value.shape[2])
    return value


def body(features, tiles, tile_row, tile_col, permutation, weight, cotangent):
    rows, width = features.shape
    side = tiles.shape[1]
    blocks = rows // side
    devices = lax.axis_size("vertex")
    here = lax.axis_index("vertex")
    base = (here * rows).astype(jnp.int32).reshape(1)
    shard = lax.axis_index("feat").astype(jnp.int32).reshape(1)
    parts = range(PARTS)
    span = rows // PARTS

    def keys(reach):
        return [(REACH + way * reach) * PARTS + p for way in ((-1, 1) if reach else (1,)) for p in parts]

    tiles = pltpu.with_memory_space_constraint(tiles, pltpu.HBM)
    ordered = [gather_rows(permutation[p * span : (p + 1) * span], base, features) for p in parts]
    plan, spans = slot_plan(tile_row, tile_col, here, blocks, devices)
    total = forward_group(keys(0), True, False, plan, spans, tiles, ordered, None)
    below, above = list(ordered), list(ordered)
    for reach in range(1, REACH + 1):
        below = [shift(b, 1) for b in below]
        above = [shift(a, -1) for a in above]
        if reach < REACH:
            below[-1], above[-1], total = lax.optimization_barrier((below[-1], above[-1], total))
        total = forward_group(keys(reach), False, reach == REACH, plan, spans, tiles, below + above, total)
    cot_full = gather_feat(cotangent)
    weight_full = gather_feat(weight)
    agg_full = gather_feat(total.reshape(rows, width))
    activations, grad, weight_terms = mix(shard, agg_full, cot_full, weight_full, side, 2 * side)
    grad_weight = sum_over_vertex(weight_terms, 8) * (1.0 / math.sqrt(rows * devices))

    carried = [None] * 2 * PARTS
    for reach in range(REACH, 0, -1):
        wanted = keys(reach)
        for p in parts:
            pair = list(backward_group([wanted[p], wanted[PARTS + p]], plan, spans, tiles, grad, bf16))
            for way in range(2):
                i = way * PARTS + p
                if reach < REACH:
                    pair[way] = add(carried[i], pair[way])
                carried[i] = shift(pair[way], (-1, 1)[way])
    own = backward_group(keys(0), plan, spans, tiles, grad, f32)
    grad_features = scatter_rows(permutation, base, own, carried[:PARTS], carried[PARTS:])
    return (activations, grad_features, grad_weight)


def solution(mesh):
    in_specs = (
        P("vertex", "feat"),
        P("vertex", None, None),
        P("vertex"),
        P("vertex"),
        P("vertex"),
        P("feat", None),
        P("vertex", "feat"),
    )
    out_specs = (P("vertex", "feat"), P("vertex", "feat"), P("feat", None))
    return jax.shard_map(body, mesh=mesh, in_specs=in_specs, out_specs=out_specs, check_vma=False)
```

```python
import functools, math
import jax, jax.numpy as jnp
from jax import lax
from jax.experimental import pallas as pl
from jax.experimental.pallas import tpu as pltpu
from jax.sharding import PartitionSpec as P

REACH = 3
PARTS = 1
ROW_PARTS = 2
GROUPS = (2 * REACH + 1) * PARTS
wide_step = 8
narrow_step = 2
ring = 32
row_bits = 5
col_bits = 5

f32 = jnp.float32
bf16 = jnp.bfloat16
SMEM = pl.BlockSpec(memory_space=pltpu.SMEM)
VMEM = pl.BlockSpec(memory_space=pltpu.VMEM)
HBM = pl.BlockSpec(memory_space=pltpu.HBM)


def near(*values):
    return [pltpu.with_memory_space_constraint(v, pltpu.VMEM) for v in values]


def group_of(offset):
    return 2 * abs(offset) - (1 if offset < 0 else 0)


def keys(*reaches):
    return [group_of(way * r) * PARTS + p for r in reaches for way in ((-1, 1) if r else (1,)) for p in range(PARTS)]


def slot_plan(tile_row, tile_col, here, blocks, devices):
    slots = tile_row.shape[0]
    owner = tile_col // blocks
    local = tile_col - owner * blocks
    span = blocks // PARTS
    part = local // span
    offset = (owner - here + devices + REACH) % devices - REACH
    even_side = (offset > 0) == (here % 2 == 0)
    group = (2 * jnp.abs(offset) - (even_side & (offset != 0)).astype(jnp.int32)) * PARTS + part
    group = jnp.where(tile_row < blocks, group, GROUPS)
    slot = jnp.arange(slots, dtype=jnp.int32)
    packed = (slot << (row_bits + col_bits)) | (tile_row << col_bits) | (local - part * span)
    same = (group[:, None] == group[None, :]) & (slot[None, :] < slot[:, None])
    rank = jnp.sum(same.astype(jnp.int32), axis=1)
    ids = jnp.arange(GROUPS, dtype=jnp.int32)
    counts = jnp.sum((group[:, None] == ids[None, :]).astype(jnp.int32), axis=0)
    steps = (counts + narrow_step - 1) // narrow_step * narrow_step
    ends = jnp.sum(jnp.where(ids[:, None] >= ids[None, :], steps[None, :], 0), axis=1)
    starts = ends - steps
    base = jnp.sum(jnp.where(group[:, None] == ids[None, :], starts[None, :], 0), axis=1)
    place = jnp.where(group < GROUPS, base + rank, -1)
    places = slots + GROUPS * narrow_step
    dummy = blocks << col_bits
    index = jnp.arange(places, dtype=jnp.int32)
    plan = dummy + jnp.sum(
        jnp.where(index[:, None] == place[None, :], packed[None, :] - dummy, 0), axis=1
    )
    return plan, jnp.concatenate([starts, ends])


def each_slot(plan, spans, tiles, buffer, sems, groups, use):
    low, high = spans[groups[0]], spans[GROUPS + groups[-1]]

    def copy(k):
        at = k & (ring - 1)
        return pltpu.make_async_copy(tiles.at[plan[k] >> (row_bits + col_bits)], buffer.at[at], sems.at[at])

    def prime(k, carry):
        copy(k).start()
        return carry

    lax.fori_loop(low, jnp.minimum(high, low + ring), prime, 0)
    for i, group in enumerate(groups):
        start, end = spans[group], spans[GROUPS + group]

        def step(k, size, i=i):
            for j in range(size):
                copy(k + j).wait()
            use(i, [plan[k + j] for j in range(size)], [buffer.at[(k + j) & (ring - 1)] for j in range(size)])

            @pl.when(k + size + ring <= high)
            def _():
                for j in range(size):
                    copy(k + j + ring).start()

            if size > narrow_step:

                @pl.when(k + size + ring > high)
                def _():
                    lax.fori_loop(k + ring, jnp.minimum(k + size + ring, high), prime, 0)

        whole = lax.div(end - start, wide_step)
        middle = start + whole * wide_step

        @pl.loop(0, whole)
        def _(s):
            step(start + s * wide_step, wide_step)

        @pl.loop(0, lax.div(end - middle, narrow_step))
        def _(s):
            step(middle + s * narrow_step, narrow_step)


def forward_kernel(groups, first, last, plan, spans, tiles, *refs):
    windows = refs[: len(groups)]
    rest = refs[len(groups) :]
    if not first:
        total_in, rest = rest[0], rest[1:]
    outs, (total, buffer, sems) = rest[:-3], rest[-3:]
    side = buffer.shape[-1]
    blocks = total.shape[0] - 1
    if first:
        total[...] = jnp.zeros_like(total)
    else:
        total[:blocks] = total_in[...]

    def use(i, packed, tile):
        values = []
        for p, t in zip(packed, tile):
            col = p & ((1 << col_bits) - 1)
            source = windows[i][pl.ds(pl.multiple_of(col * side, side), side), :]
            values.append(jnp.dot(t[...], source, preferred_element_type=f32))
        for p, value in zip(packed, values):
            total[(p >> col_bits) & ((1 << row_bits) - 1)] += value

    each_slot(plan, spans, tiles, buffer, sems, groups, use)
    share = blocks // len(outs)
    for p, out in enumerate(outs):
        out[...] = total[p * share : (p + 1) * share].astype(out.dtype)


def forward_group(groups, first, last, plan, spans, tiles, windows, total):
    side = tiles.shape[-1]
    blocks = PARTS * windows[0].shape[0] // side
    shape = (blocks, side, windows[0].shape[1])
    return pl.pallas_call(
        functools.partial(forward_kernel, groups, first, last),
        out_shape=[pltpu.VMEM((blocks // ROW_PARTS, *shape[1:]), bf16)] * ROW_PARTS if last else [pltpu.VMEM(shape, f32)],
        in_specs=[SMEM, SMEM, HBM] + [VMEM] * (len(groups) + (not first)),
        out_specs=[VMEM] * (ROW_PARTS if last else 1),
        scratch_shapes=[
            pltpu.VMEM((blocks + 1, *shape[1:]), f32),
            pltpu.VMEM((ring, side, side), bf16),
            pltpu.SemaphoreType.DMA((ring,)),
        ],
        cost_estimate=pl.CostEstimate(
            flops=len(groups) * 30 * 2**22, bytes_accessed=len(groups) * 30 * 2**15, transcendentals=0
        ),
        compiler_params=pltpu.CompilerParams(vmem_limit_bytes=16 * 2**20),
        name="forward_group",
    )(plan, spans, tiles, *near(*windows, *([] if first else [total])))


def backward_kernel(groups, plan, spans, tiles, *refs):
    outs = refs[ROW_PARTS:-4]
    grad, total, buffer, sems = refs[-4:]
    blocks = grad.shape[0]
    share = blocks // ROW_PARTS
    for p in range(ROW_PARTS):
        grad[p * share : (p + 1) * share] = refs[p][...]
    span = blocks // PARTS
    total[...] = jnp.zeros_like(total)

    def use(i, packed, tile):
        values = []
        for p, t in zip(packed, tile):
            row = (p >> col_bits) & ((1 << row_bits) - 1)
            values.append(jnp.dot(grad[jnp.minimum(row, blocks - 1)], t[...], preferred_element_type=f32))
        for p, value in zip(packed, values):
            row = (p >> col_bits) & ((1 << row_bits) - 1)
            col = i * span + (p & ((1 << col_bits) - 1))
            total[jnp.where(row == blocks, total.shape[0] - 1, col)] += value

    each_slot(plan, spans, tiles, buffer, sems, groups, use)
    for o, out in enumerate(outs):
        out[...] = total[o * span : (o + 1) * span].astype(out.dtype)


def backward_group(groups, plan, spans, tiles, grads, dtypes):
    blocks, width, side = grads[0].shape
    blocks = blocks * ROW_PARTS
    shape = (blocks, width, side)
    part = (blocks // PARTS, width, side)
    return pl.pallas_call(
        functools.partial(backward_kernel, groups),
        out_shape=[pltpu.VMEM(part, d) for d in dtypes],
        in_specs=[SMEM, SMEM, HBM] + [VMEM] * ROW_PARTS,
        out_specs=[VMEM] * len(dtypes),
        scratch_shapes=[
            pltpu.VMEM(shape, bf16),
            pltpu.VMEM((len(dtypes) * part[0] + 1, width, side), f32),
            pltpu.VMEM((ring, side, side), bf16),
            pltpu.SemaphoreType.DMA((ring,)),
        ],
        cost_estimate=pl.CostEstimate(
            flops=len(groups) * 30 * 2**22, bytes_accessed=len(groups) * 30 * 2**15, transcendentals=0
        ),
        compiler_params=pltpu.CompilerParams(vmem_limit_bytes=16 * 2**20),
        name="backward_group",
    )(plan, spans, tiles, *near(*grads))


def swap(value, first):
    count = lax.axis_size("vertex")
    pairs = []
    for low in range(first, count + first, 2):
        pairs += [(low % count, (low + 1) % count), ((low + 1) % count, low % count)]
    return lax.ppermute(value, "vertex", pairs)


def exchange(value, step):
    count = lax.axis_size("feat")
    return lax.ppermute(value, "feat", [(source, source ^ step) for source in range(count)])


def gather_feat(value):
    far = exchange(value, 2)
    return [value, exchange(value, 1), far, exchange(far, 1)]


def gather_kernel(part, perm, base, source, out, wide, moved):
    rows = out.shape[0]
    wide[...] = source[...].astype(f32)
    first = base[0]

    @pl.loop(0, rows // 16)
    def _(step):
        at = step * 16
        for j in range(16):
            moved[pl.ds(at + j, 1), :] = wide[pl.ds(perm[part * rows + at + j] - first, 1), :]

    out[...] = moved[...].astype(out.dtype)


def gather_rows(part, perm, base, source):
    shape = (perm.shape[0] // PARTS, source.shape[1])
    return pl.pallas_call(
        functools.partial(gather_kernel, part),
        out_shape=pltpu.VMEM(shape, source.dtype),
        in_specs=[SMEM, SMEM, VMEM],
        out_specs=VMEM,
        scratch_shapes=[pltpu.VMEM(source.shape, f32), pltpu.VMEM(shape, f32)],
        cost_estimate=pl.CostEstimate(flops=0, bytes_accessed=12 * 2**20, transcendentals=0),
        compiler_params=pltpu.CompilerParams(vmem_limit_bytes=8 * 2**20),
        name="gather_rows",
    )(perm, base, source)


def mix_kernel(part, block_rows, shard, *refs):
    agg, cot, weight = refs[0:4], refs[4:8], refs[8:12]
    act, grad_agg, grad_weight, full, total = refs[-5:]
    rows, width = agg[1].shape
    columns = [pl.ds(pl.multiple_of((shard[0] ^ k) * width, width), width) for k in range(4)]
    for i in range(4):
        for k, c in enumerate(columns):
            full[i * width : (i + 1) * width, k * width : (k + 1) * width] = weight[i][:, c]
    total[...] = jnp.zeros_like(total)
    side = grad_agg.shape[2]

    @pl.loop(0, rows // block_rows)
    def _(step):
        here = pl.ds(pl.multiple_of(step * block_rows, block_rows), block_rows)
        whole = pl.ds(pl.multiple_of(part * rows + step * block_rows, block_rows), block_rows)
        mine = agg[0][here, :]
        mixed = jnp.dot(
            jnp.concatenate([a[here, :] for a in agg], axis=1), full[...], preferred_element_type=f32
        )
        sig = 0.5 + 0.5 * jnp.tanh(0.5 * mixed)
        cotangent = jnp.concatenate([c[whole, :] for c in cot], axis=1).astype(f32)
        grad = (cotangent * sig * (1.0 + mixed * (1.0 - sig))).astype(bf16)
        act[here, :] = (mixed[:, :width] * sig[:, :width]).astype(bf16)
        back = lax.dot_general(full[:width, :], grad, (((1,), (1,)), ((), ())), preferred_element_type=f32)
        for b in range(block_rows // side):
            grad_agg[step * (block_rows // side) + b] = back[:, b * side : (b + 1) * side].astype(bf16)
        total[...] += lax.dot_general(mine, grad, (((0,), (0,)), ((), ())), preferred_element_type=f32)

    for k in range(4):
        grad_weight[shard[0] ^ k] = total[:, k * width : (k + 1) * width]


def mix(part, shard, agg, cot, weight, side, block_rows):
    rows, width = agg[1].shape
    full = weight[0].shape[1]
    return pl.pallas_call(
        functools.partial(mix_kernel, part, block_rows),
        out_shape=[
            jax.ShapeDtypeStruct((rows, width), bf16),
            pltpu.VMEM((rows // side, width, side), bf16),
            pltpu.VMEM((full // width, width, width), f32),
        ],
        in_specs=[SMEM] + [VMEM] * 12,
        out_specs=[VMEM] * 3,
        scratch_shapes=[pltpu.VMEM((full, full), bf16), pltpu.VMEM((width, full), f32)],
        cost_estimate=pl.CostEstimate(
            flops=3 * rows * full * full, bytes_accessed=8 * rows * full, transcendentals=rows * full
        ),
        compiler_params=pltpu.CompilerParams(vmem_limit_bytes=16 * 2**20),
        name="mix",
    )(shard, *near(*agg, *cot), *weight)


def add_kernel(carried, own, out):
    out[...] = (carried[...].astype(f32) + own[...].astype(f32)).astype(bf16)


def add_part(carried, own):
    return pl.pallas_call(
        add_kernel,
        out_shape=pltpu.VMEM(carried.shape, bf16),
        in_specs=[VMEM] * 2,
        out_specs=VMEM,
        cost_estimate=pl.CostEstimate(flops=0, bytes_accessed=6 * carried.size, transcendentals=0),
        compiler_params=pltpu.CompilerParams(vmem_limit_bytes=4 * 2**20),
        name="add_part",
    )(*near(carried, own))


def scatter_kernel(perm, base, own, left, right, out, moved, wide):
    first = base[0]
    blocks, width, side = own.shape

    @pl.loop(0, blocks)
    def _(b):
        total = own[b] + left[b].astype(f32) + right[b].astype(f32)
        wide[...] = total.T
        at = b * side
        for j in range(side):
            moved[pl.ds(perm[at + j] - first, 1), :] = wide[j : j + 1, :]

    out[...] = moved[...].astype(out.dtype)


def scatter_rows(perm, base, own, left, right):
    width = own.shape[1]
    rows = perm.shape[0]
    return pl.pallas_call(
        scatter_kernel,
        out_shape=jax.ShapeDtypeStruct((rows, width), bf16),
        in_specs=[SMEM, SMEM] + [VMEM] * 3,
        out_specs=VMEM,
        scratch_shapes=[pltpu.VMEM((rows, width), f32), pltpu.VMEM((own.shape[2], width), f32)],
        cost_estimate=pl.CostEstimate(flops=0, bytes_accessed=12 * 2**20, transcendentals=0),
        compiler_params=pltpu.CompilerParams(vmem_limit_bytes=8 * 2**20),
        name="scatter_rows",
    )(perm, base, *near(own, left, right))


def sum_share(value):
    split = value.reshape(lax.axis_size("vertex"), -1, value.shape[-1])
    return jnp.sum(lax.all_to_all(split, "vertex", 0, 0, tiled=True), axis=0)


def spread_shares(mine, scale):
    spread = jnp.broadcast_to((mine * scale)[None], (lax.axis_size("vertex"), *mine.shape))
    return lax.all_to_all(spread, "vertex", 0, 0, tiled=True)


def body(features, tiles, tile_row, tile_col, permutation, weight, cotangent):
    rows, width = features.shape
    side = tiles.shape[1]
    blocks = rows // side
    devices = lax.axis_size("vertex")
    here = lax.axis_index("vertex")
    base = (here * rows).astype(jnp.int32).reshape(1)
    shard = lax.axis_index("feat").astype(jnp.int32).reshape(1)
    span = rows // ROW_PARTS
    scale = 1.0 / math.sqrt(rows * devices)
    tiles = pltpu.with_memory_space_constraint(tiles, pltpu.HBM)

    far = exchange(cotangent, 2)
    weight_far = exchange(weight, 2)
    ordered = gather_rows(0, permutation, base, features)
    plan, spans = slot_plan(tile_row, tile_col, here, blocks, devices)
    ordered, far, weight_far = lax.optimization_barrier((ordered, far, weight_far))

    even, odd = swap(ordered, 0), swap(ordered, 1)
    windows = [ordered, even, odd]
    weight_full = [weight, exchange(weight, 1), weight_far, exchange(weight_far, 1)]
    cot_full = [cotangent, exchange(cotangent, 1), far, exchange(far, 1)]
    for reach in range(2, REACH + 1):
        even, odd, plan = lax.optimization_barrier((even, odd, plan))
        even, odd = swap(odd, 0), swap(even, 1)
        windows += [even, odd]
    (total,) = forward_group(keys(*range(REACH)), True, False, plan, spans, tiles, windows[:-2], None)
    total, weight_full, cot_full = lax.optimization_barrier((total, weight_full, cot_full))
    total = forward_group(keys(REACH), False, True, plan, spans, tiles, windows[-2:], total)
    aggregated = [t.reshape(span, width) for t in total]

    acts, grads, terms = [], [], []
    for p in range(ROW_PARTS):
        act, grad, term = mix(p, shard, gather_feat(aggregated[p]), cot_full, weight_full, side, 2 * side)
        acts.append(act)
        grads.append(grad)
        terms.append(term)
    activations = jnp.concatenate(acts, axis=0)

    def after(token, value):
        return lax.optimization_barrier((exchange(token[0, :16], 1), value))[1]

    even, odd = backward_group(keys(REACH), plan, spans, tiles, grads, [bf16] * 2)
    share = sum_share(after(even, sum(terms)))
    even, odd = swap(even, 0), swap(odd, 1)
    own = backward_group(keys(2), plan, spans, tiles, grads, [bf16] * 2)
    even, odd, plan = lax.optimization_barrier((even, odd, plan))
    even, odd = add_part(odd, own[0]), add_part(even, own[1])
    even, odd = swap(even, 0), swap(odd, 1)
    own = backward_group(keys(0, 1), plan, spans, tiles, grads, [f32] + [bf16] * 2)
    even, odd = add_part(odd, own[1]), add_part(even, own[2])
    share = spread_shares(after(even, share), scale)
    even, odd = swap(even, 0), swap(odd, 1)
    even, odd, activations = lax.optimization_barrier((even, odd, activations))
    grad_features = scatter_rows(permutation, base, own[0], even, odd)
    share = share.reshape(-1, width, width)
    grad_weight = jnp.concatenate([share[k] for k in range(share.shape[0])], axis=1)
    return (activations, grad_features, grad_weight)


def solution(mesh):
    in_specs = (
        P("vertex", "feat"),
        P("vertex", None, None),
        P("vertex"),
        P("vertex"),
        P("vertex"),
        P("feat", None),
        P("vertex", "feat"),
    )
    out_specs = (P("vertex", "feat"), P("vertex", "feat"), P("feat", None))
    return jax.shard_map(body, mesh=mesh, in_specs=in_specs, out_specs=out_specs, check_vma=False)
```

```python
import functools, math
import jax, jax.numpy as jnp
from jax import lax
from jax.experimental import pallas as pl
from jax.experimental.pallas import tpu as pltpu
from jax.sharding import PartitionSpec as P

REACH = 3
PARTS = 1
ROW_PARTS = 2
GROUPS = (2 * REACH + 1) * PARTS
wide_step = 8
narrow_step = 2
ring = 32
row_bits = 5
col_bits = 5

f32 = jnp.float32
bf16 = jnp.bfloat16
SMEM = pl.BlockSpec(memory_space=pltpu.SMEM)
VMEM = pl.BlockSpec(memory_space=pltpu.VMEM)
HBM = pl.BlockSpec(memory_space=pltpu.HBM)


def near(*values):
    return [pltpu.with_memory_space_constraint(v, pltpu.VMEM) for v in values]


def group_of(offset):
    return 2 * abs(offset) - (1 if offset < 0 else 0)


def keys(*reaches):
    return [group_of(way * r) * PARTS + p for r in reaches for way in ((-1, 1) if r else (1,)) for p in range(PARTS)]


def slot_plan(tile_row, tile_col, here, blocks, devices):
    slots = tile_row.shape[0]
    owner = tile_col // blocks
    local = tile_col - owner * blocks
    span = blocks // PARTS
    part = local // span
    offset = (owner - here + devices + REACH) % devices - REACH
    even_side = (offset > 0) == (here % 2 == 0)
    group = (2 * jnp.abs(offset) - (even_side & (offset != 0)).astype(jnp.int32)) * PARTS + part
    group = jnp.where(tile_row < blocks, group, GROUPS)
    slot = jnp.arange(slots, dtype=jnp.int32)
    packed = (slot << (row_bits + col_bits)) | (tile_row << col_bits) | (local - part * span)
    same = (group[:, None] == group[None, :]) & (slot[None, :] < slot[:, None])
    rank = jnp.sum(same.astype(jnp.int32), axis=1)
    ids = jnp.arange(GROUPS, dtype=jnp.int32)
    counts = jnp.sum((group[:, None] == ids[None, :]).astype(jnp.int32), axis=0)
    steps = (counts + narrow_step - 1) // narrow_step * narrow_step
    ends = jnp.sum(jnp.where(ids[:, None] >= ids[None, :], steps[None, :], 0), axis=1)
    starts = ends - steps
    base = jnp.sum(jnp.where(group[:, None] == ids[None, :], starts[None, :], 0), axis=1)
    place = jnp.where(group < GROUPS, base + rank, -1)
    places = slots + GROUPS * narrow_step
    dummy = blocks << col_bits
    index = jnp.arange(places, dtype=jnp.int32)
    plan = dummy + jnp.sum(
        jnp.where(index[:, None] == place[None, :], packed[None, :] - dummy, 0), axis=1
    )
    return plan, jnp.concatenate([starts, ends])


def each_slot(plan, spans, tiles, buffer, sems, groups, use):
    low, high = spans[groups[0]], spans[GROUPS + groups[-1]]

    def copy(k):
        at = k & (ring - 1)
        return pltpu.make_async_copy(tiles.at[plan[k] >> (row_bits + col_bits)], buffer.at[at], sems.at[at])

    def prime(k, carry):
        copy(k).start()
        return carry

    lax.fori_loop(low, jnp.minimum(high, low + ring), prime, 0)
    for i, group in enumerate(groups):
        start, end = spans[group], spans[GROUPS + group]

        def step(k, size, i=i):
            for j in range(size):
                copy(k + j).wait()
            use(i, [plan[k + j] for j in range(size)], [buffer.at[(k + j) & (ring - 1)] for j in range(size)])

            @pl.when(k + size + ring <= high)
            def _():
                for j in range(size):
                    copy(k + j + ring).start()

            if size > narrow_step:

                @pl.when(k + size + ring > high)
                def _():
                    lax.fori_loop(k + ring, jnp.minimum(k + size + ring, high), prime, 0)

        whole = lax.div(end - start, wide_step)
        middle = start + whole * wide_step

        @pl.loop(0, whole)
        def _(s):
            step(start + s * wide_step, wide_step)

        @pl.loop(0, lax.div(end - middle, narrow_step))
        def _(s):
            step(middle + s * narrow_step, narrow_step)


def forward_kernel(groups, first, last, plan, spans, tiles, *refs):
    windows = refs[: len(groups)]
    rest = refs[len(groups) :]
    if not first:
        total_in, rest = rest[0], rest[1:]
    outs, (total, buffer, sems) = rest[:-3], rest[-3:]
    side = buffer.shape[-1]
    blocks = total.shape[0] - 1
    if first:
        total[...] = jnp.zeros_like(total)
    else:
        total[:blocks] = total_in[...]

    def use(i, packed, tile):
        values = []
        for p, t in zip(packed, tile):
            col = p & ((1 << col_bits) - 1)
            source = windows[i][pl.ds(pl.multiple_of(col * side, side), side), :]
            values.append(jnp.dot(t[...], source, preferred_element_type=f32))
        for p, value in zip(packed, values):
            total[(p >> col_bits) & ((1 << row_bits) - 1)] += value

    each_slot(plan, spans, tiles, buffer, sems, groups, use)
    share = blocks // len(outs)
    for p, out in enumerate(outs):
        out[...] = total[p * share : (p + 1) * share].astype(out.dtype)


def forward_group(groups, first, last, plan, spans, tiles, windows, total):
    side = tiles.shape[-1]
    blocks = PARTS * windows[0].shape[0] // side
    shape = (blocks, side, windows[0].shape[1])
    return pl.pallas_call(
        functools.partial(forward_kernel, groups, first, last),
        out_shape=[pltpu.VMEM((blocks // ROW_PARTS, *shape[1:]), bf16)] * ROW_PARTS if last else [pltpu.VMEM(shape, f32)],
        in_specs=[SMEM, SMEM, HBM] + [VMEM] * (len(groups) + (not first)),
        out_specs=[VMEM] * (ROW_PARTS if last else 1),
        scratch_shapes=[
            pltpu.VMEM((blocks + 1, *shape[1:]), f32),
            pltpu.VMEM((ring, side, side), bf16),
            pltpu.SemaphoreType.DMA((ring,)),
        ],
        cost_estimate=pl.CostEstimate(
            flops=len(groups) * 30 * 2**22, bytes_accessed=len(groups) * 30 * 2**15, transcendentals=0
        ),
        compiler_params=pltpu.CompilerParams(vmem_limit_bytes=16 * 2**20),
        name="forward_group",
    )(plan, spans, tiles, *near(*windows, *([] if first else [total])))


def backward_kernel(groups, plan, spans, tiles, *refs):
    outs = refs[ROW_PARTS:-4]
    grad, total, buffer, sems = refs[-4:]
    blocks = grad.shape[0]
    share = blocks // ROW_PARTS
    for p in range(ROW_PARTS):
        grad[p * share : (p + 1) * share] = refs[p][...]
    span = blocks // PARTS
    total[...] = jnp.zeros_like(total)

    def use(i, packed, tile):
        values = []
        for p, t in zip(packed, tile):
            row = (p >> col_bits) & ((1 << row_bits) - 1)
            values.append(jnp.dot(grad[jnp.minimum(row, blocks - 1)], t[...], preferred_element_type=f32))
        for p, value in zip(packed, values):
            row = (p >> col_bits) & ((1 << row_bits) - 1)
            col = i * span + (p & ((1 << col_bits) - 1))
            total[jnp.where(row == blocks, total.shape[0] - 1, col)] += value

    each_slot(plan, spans, tiles, buffer, sems, groups, use)
    for o, out in enumerate(outs):
        out[...] = total[o * span : (o + 1) * span].astype(out.dtype)


def backward_group(groups, plan, spans, tiles, grads, dtypes):
    blocks, width, side = grads[0].shape
    blocks = blocks * ROW_PARTS
    shape = (blocks, width, side)
    part = (blocks // PARTS, width, side)
    return pl.pallas_call(
        functools.partial(backward_kernel, groups),
        out_shape=[pltpu.VMEM(part, d) for d in dtypes],
        in_specs=[SMEM, SMEM, HBM] + [VMEM] * ROW_PARTS,
        out_specs=[VMEM] * len(dtypes),
        scratch_shapes=[
            pltpu.VMEM(shape, bf16),
            pltpu.VMEM((len(dtypes) * part[0] + 1, width, side), f32),
            pltpu.VMEM((ring, side, side), bf16),
            pltpu.SemaphoreType.DMA((ring,)),
        ],
        cost_estimate=pl.CostEstimate(
            flops=len(groups) * 30 * 2**22, bytes_accessed=len(groups) * 30 * 2**15, transcendentals=0
        ),
        compiler_params=pltpu.CompilerParams(vmem_limit_bytes=16 * 2**20),
        name="backward_group",
    )(plan, spans, tiles, *near(*grads))


def swap(value, first):
    count = lax.axis_size("vertex")
    pairs = []
    for low in range(first, count + first, 2):
        pairs += [(low % count, (low + 1) % count), ((low + 1) % count, low % count)]
    return lax.ppermute(value, "vertex", pairs)


def exchange(value, step):
    count = lax.axis_size("feat")
    return lax.ppermute(value, "feat", [(source, source ^ step) for source in range(count)])


def gather_feat(value):
    far = exchange(value, 2)
    return [value, exchange(value, 1), far, exchange(far, 1)]


def gather_kernel(part, perm, base, source, out, wide, moved):
    rows = out.shape[0]
    wide[...] = source[...].astype(f32)
    first = base[0]

    @pl.loop(0, rows // 16)
    def _(step):
        at = step * 16
        for j in range(16):
            moved[pl.ds(at + j, 1), :] = wide[pl.ds(perm[part * rows + at + j] - first, 1), :]

    out[...] = moved[...].astype(out.dtype)


def gather_rows(part, perm, base, source):
    shape = (perm.shape[0] // PARTS, source.shape[1])
    return pl.pallas_call(
        functools.partial(gather_kernel, part),
        out_shape=pltpu.VMEM(shape, source.dtype),
        in_specs=[SMEM, SMEM, VMEM],
        out_specs=VMEM,
        scratch_shapes=[pltpu.VMEM(source.shape, f32), pltpu.VMEM(shape, f32)],
        cost_estimate=pl.CostEstimate(flops=0, bytes_accessed=12 * 2**20, transcendentals=0),
        compiler_params=pltpu.CompilerParams(vmem_limit_bytes=8 * 2**20),
        name="gather_rows",
    )(perm, base, source)


def mix_kernel(part, block_rows, shard, *refs):
    agg, cot, weight = refs[0:4], refs[4:8], refs[8:12]
    act, grad_agg, grad_weight, full, total = refs[-5:]
    rows, width = agg[1].shape
    columns = [pl.ds(pl.multiple_of((shard[0] ^ k) * width, width), width) for k in range(4)]
    for i in range(4):
        for k, c in enumerate(columns):
            full[i * width : (i + 1) * width, k * width : (k + 1) * width] = weight[i][:, c]
    total[...] = jnp.zeros_like(total)
    side = grad_agg.shape[2]

    @pl.loop(0, rows // block_rows)
    def _(step):
        here = pl.ds(pl.multiple_of(step * block_rows, block_rows), block_rows)
        whole = pl.ds(pl.multiple_of(part * rows + step * block_rows, block_rows), block_rows)
        mine = agg[0][here, :]
        mixed = jnp.dot(
            jnp.concatenate([a[here, :] for a in agg], axis=1), full[...], preferred_element_type=f32
        )
        sig = 0.5 + 0.5 * jnp.tanh(0.5 * mixed)
        cotangent = jnp.concatenate([c[whole, :] for c in cot], axis=1).astype(f32)
        grad = (cotangent * sig * (1.0 + mixed * (1.0 - sig))).astype(bf16)
        act[here, :] = (mixed[:, :width] * sig[:, :width]).astype(bf16)
        back = lax.dot_general(full[:width, :], grad, (((1,), (1,)), ((), ())), preferred_element_type=f32)
        for b in range(block_rows // side):
            grad_agg[step * (block_rows // side) + b] = back[:, b * side : (b + 1) * side].astype(bf16)
        total[...] += lax.dot_general(mine, grad, (((0,), (0,)), ((), ())), preferred_element_type=f32)

    for k in range(4):
        grad_weight[shard[0] ^ k] = total[:, k * width : (k + 1) * width]


def mix(part, shard, agg, cot, weight, side, block_rows):
    rows, width = agg[1].shape
    full = weight[0].shape[1]
    return pl.pallas_call(
        functools.partial(mix_kernel, part, block_rows),
        out_shape=[
            jax.ShapeDtypeStruct((rows, width), bf16),
            pltpu.VMEM((rows // side, width, side), bf16),
            pltpu.VMEM((full // width, width, width), f32),
        ],
        in_specs=[SMEM] + [VMEM] * 12,
        out_specs=[VMEM] * 3,
        scratch_shapes=[pltpu.VMEM((full, full), bf16), pltpu.VMEM((width, full), f32)],
        cost_estimate=pl.CostEstimate(
            flops=3 * rows * full * full, bytes_accessed=8 * rows * full, transcendentals=rows * full
        ),
        compiler_params=pltpu.CompilerParams(vmem_limit_bytes=16 * 2**20),
        name="mix",
    )(shard, *near(*agg, *cot), *weight)


def add_kernel(carried, own, out):
    out[...] = (carried[...].astype(f32) + own[...].astype(f32)).astype(bf16)


def add_part(carried, own):
    return pl.pallas_call(
        add_kernel,
        out_shape=pltpu.VMEM(carried.shape, bf16),
        in_specs=[VMEM] * 2,
        out_specs=VMEM,
        cost_estimate=pl.CostEstimate(flops=0, bytes_accessed=6 * carried.size, transcendentals=0),
        compiler_params=pltpu.CompilerParams(vmem_limit_bytes=4 * 2**20),
        name="add_part",
    )(*near(carried, own))


def scatter_kernel(perm, base, own, left, right, out, moved, wide):
    first = base[0]
    blocks, width, side = own.shape

    @pl.loop(0, blocks)
    def _(b):
        total = own[b] + left[b].astype(f32) + right[b].astype(f32)
        wide[...] = total.T
        at = b * side
        for j in range(side):
            moved[pl.ds(perm[at + j] - first, 1), :] = wide[j : j + 1, :]

    out[...] = moved[...].astype(out.dtype)


def scatter_rows(perm, base, own, left, right):
    width = own.shape[1]
    rows = perm.shape[0]
    return pl.pallas_call(
        scatter_kernel,
        out_shape=jax.ShapeDtypeStruct((rows, width), bf16),
        in_specs=[SMEM, SMEM] + [VMEM] * 3,
        out_specs=VMEM,
        scratch_shapes=[pltpu.VMEM((rows, width), f32), pltpu.VMEM((own.shape[2], width), f32)],
        cost_estimate=pl.CostEstimate(flops=0, bytes_accessed=12 * 2**20, transcendentals=0),
        compiler_params=pltpu.CompilerParams(vmem_limit_bytes=8 * 2**20),
        name="scatter_rows",
    )(perm, base, *near(own, left, right))


def sum_share(value):
    split = value.reshape(lax.axis_size("vertex"), -1, value.shape[-1])
    return jnp.sum(lax.all_to_all(split, "vertex", 0, 0, tiled=True), axis=0)


def spread_shares(mine, scale):
    spread = jnp.broadcast_to((mine * scale)[None], (lax.axis_size("vertex"), *mine.shape))
    return lax.all_to_all(spread, "vertex", 0, 0, tiled=True)


def body(features, tiles, tile_row, tile_col, permutation, weight, cotangent):
    rows, width = features.shape
    side = tiles.shape[1]
    blocks = rows // side
    devices = lax.axis_size("vertex")
    here = lax.axis_index("vertex")
    base = (here * rows).astype(jnp.int32).reshape(1)
    shard = lax.axis_index("feat").astype(jnp.int32).reshape(1)
    span = rows // ROW_PARTS
    scale = 1.0 / math.sqrt(rows * devices)
    tiles = pltpu.with_memory_space_constraint(tiles, pltpu.HBM)

    far = exchange(cotangent, 2)
    weight_far = exchange(weight, 2)
    ordered = gather_rows(0, permutation, base, features)
    plan, spans = slot_plan(tile_row, tile_col, here, blocks, devices)
    ordered, far, weight_far = lax.optimization_barrier((ordered, far, weight_far))

    even, odd = swap(ordered, 0), swap(ordered, 1)
    windows = [ordered, even, odd]
    weight_full = [weight, exchange(weight, 1), weight_far, exchange(weight_far, 1)]
    cot_full = [cotangent, exchange(cotangent, 1), far, exchange(far, 1)]
    for reach in range(2, REACH + 1):
        even, odd, plan = lax.optimization_barrier((even, odd, plan))
        even, odd = swap(odd, 0), swap(even, 1)
        windows += [even, odd]
    (total,) = forward_group(keys(*range(REACH)), True, False, plan, spans, tiles, windows[:-2], None)
    total, weight_full, cot_full = lax.optimization_barrier((total, weight_full, cot_full))
    total = forward_group(keys(REACH), False, True, plan, spans, tiles, windows[-2:], total)
    aggregated = [t.reshape(span, width) for t in total]

    acts, grads, terms = [], [], []
    for p in range(ROW_PARTS):
        act, grad, term = mix(p, shard, gather_feat(aggregated[p]), cot_full, weight_full, side, 6 * side)
        acts.append(act)
        grads.append(grad)
        terms.append(term)
    activations = jnp.concatenate(acts, axis=0)

    def after(token, value):
        return lax.optimization_barrier((exchange(token[0, :16], 1), value))[1]

    even, odd = backward_group(keys(REACH), plan, spans, tiles, grads, [bf16] * 2)
    share = sum_share(after(even, sum(terms)))
    even, odd = swap(even, 0), swap(odd, 1)
    own = backward_group(keys(2), plan, spans, tiles, grads, [bf16] * 2)
    even, odd, plan = lax.optimization_barrier((even, odd, plan))
    even, odd = add_part(odd, own[0]), add_part(even, own[1])
    even, odd = swap(even, 0), swap(odd, 1)
    own = backward_group(keys(0, 1), plan, spans, tiles, grads, [f32] + [bf16] * 2)
    even, odd = add_part(odd, own[1]), add_part(even, own[2])
    share = spread_shares(after(even, share), scale)
    even, odd = swap(even, 0), swap(odd, 1)
    even, odd, activations = lax.optimization_barrier((even, odd, activations))
    grad_features = scatter_rows(permutation, base, own[0], even, odd)
    share = share.reshape(-1, width, width)
    grad_weight = jnp.concatenate([share[k] for k in range(share.shape[0])], axis=1)
    return (activations, grad_features, grad_weight)


def solution(mesh):
    in_specs = (
        P("vertex", "feat"),
        P("vertex", None, None),
        P("vertex"),
        P("vertex"),
        P("vertex"),
        P("feat", None),
        P("vertex", "feat"),
    )
    out_specs = (P("vertex", "feat"), P("vertex", "feat"), P("feat", None))
    return jax.shard_map(body, mesh=mesh, in_specs=in_specs, out_specs=out_specs, check_vma=False)
```

```python
import functools, math
import jax, jax.numpy as jnp
from jax import lax
from jax.experimental import pallas as pl
from jax.experimental.pallas import tpu as pltpu
from jax.sharding import PartitionSpec as P

REACH = 3
PARTS = 1
ROW_PARTS = 2
GROUPS = (2 * REACH + 1) * PARTS
wide_step = 8
together = 4
narrow_step = 2
ring = 32
row_bits = 5
col_bits = 5

f32 = jnp.float32
bf16 = jnp.bfloat16
SMEM = pl.BlockSpec(memory_space=pltpu.SMEM)
VMEM = pl.BlockSpec(memory_space=pltpu.VMEM)
HBM = pl.BlockSpec(memory_space=pltpu.HBM)


def near(*values):
    return [pltpu.with_memory_space_constraint(v, pltpu.VMEM) for v in values]


def group_of(offset):
    return 2 * abs(offset) - (1 if offset < 0 else 0)


def keys(*reaches):
    return [group_of(way * r) * PARTS + p for r in reaches for way in ((-1, 1) if r else (1,)) for p in range(PARTS)]


def slot_plan(tile_row, tile_col, here, blocks, devices):
    slots = tile_row.shape[0]
    owner = tile_col // blocks
    local = tile_col - owner * blocks
    span = blocks // PARTS
    part = local // span
    offset = (owner - here + devices + REACH) % devices - REACH
    even_side = (offset > 0) == (here % 2 == 0)
    group = (2 * jnp.abs(offset) - (even_side & (offset != 0)).astype(jnp.int32)) * PARTS + part
    group = jnp.where(tile_row < blocks, group, GROUPS)
    slot = jnp.arange(slots, dtype=jnp.int32)
    packed = (slot << (row_bits + col_bits)) | (tile_row << col_bits) | (local - part * span)
    same = (group[:, None] == group[None, :]) & (slot[None, :] < slot[:, None])
    rank = jnp.sum(same.astype(jnp.int32), axis=1)
    ids = jnp.arange(GROUPS, dtype=jnp.int32)
    counts = jnp.sum((group[:, None] == ids[None, :]).astype(jnp.int32), axis=0)
    steps = (counts + narrow_step - 1) // narrow_step * narrow_step
    ends = jnp.sum(jnp.where(ids[:, None] >= ids[None, :], steps[None, :], 0), axis=1)
    starts = ends - steps
    base = jnp.sum(jnp.where(group[:, None] == ids[None, :], starts[None, :], 0), axis=1)
    place = jnp.where(group < GROUPS, base + rank, -1)
    places = slots + GROUPS * narrow_step
    dummy = blocks << col_bits
    index = jnp.arange(places, dtype=jnp.int32)
    plan = dummy + jnp.sum(
        jnp.where(index[:, None] == place[None, :], packed[None, :] - dummy, 0), axis=1
    )
    return plan, jnp.concatenate([starts, ends])


def each_slot(plan, spans, tiles, buffer, sems, groups, use):
    low, high = spans[groups[0]], spans[GROUPS + groups[-1]]

    def copy(k):
        at = k & (ring - 1)
        return pltpu.make_async_copy(tiles.at[plan[k] >> (row_bits + col_bits)], buffer.at[at], sems.at[at])

    def prime(k, carry):
        copy(k).start()
        return carry

    lax.fori_loop(low, jnp.minimum(high, low + ring), prime, 0)
    for i, group in enumerate(groups):
        start, end = spans[group], spans[GROUPS + group]

        def step(k, size, i=i):
            for j in range(size):
                copy(k + j).wait()
            use(i, [plan[k + j] for j in range(size)], [buffer.at[(k + j) & (ring - 1)] for j in range(size)])

            @pl.when(k + size + ring <= high)
            def _():
                for j in range(size):
                    copy(k + j + ring).start()

            if size > narrow_step:

                @pl.when(k + size + ring > high)
                def _():
                    lax.fori_loop(k + ring, jnp.minimum(k + size + ring, high), prime, 0)

        whole = lax.div(end - start, wide_step)
        middle = start + whole * wide_step

        @pl.loop(0, whole)
        def _(s):
            step(start + s * wide_step, wide_step)

        @pl.loop(0, lax.div(end - middle, narrow_step))
        def _(s):
            step(middle + s * narrow_step, narrow_step)


def forward_kernel(groups, first, last, plan, spans, tiles, *refs):
    windows = refs[: len(groups)]
    rest = refs[len(groups) :]
    if not first:
        total_in, rest = rest[0], rest[1:]
    outs, (total, buffer, sems) = rest[:-3], rest[-3:]
    side = buffer.shape[-1]
    blocks = total.shape[0] - 1
    if first:
        total[...] = jnp.zeros_like(total)
    else:
        total[:blocks] = total_in[...]

    def use(i, packed, tile):
        values = []
        for p, t in zip(packed, tile):
            col = p & ((1 << col_bits) - 1)
            source = windows[i][pl.ds(pl.multiple_of(col * side, side), side), :]
            values.append(jnp.dot(t[...], source, preferred_element_type=f32))
        for p, value in zip(packed, values):
            total[(p >> col_bits) & ((1 << row_bits) - 1)] += value

    each_slot(plan, spans, tiles, buffer, sems, groups, use)
    share = blocks // len(outs)
    for p, out in enumerate(outs):
        out[...] = total[p * share : (p + 1) * share].astype(out.dtype)


def forward_group(groups, first, last, plan, spans, tiles, windows, total):
    side = tiles.shape[-1]
    blocks = PARTS * windows[0].shape[0] // side
    shape = (blocks, side, windows[0].shape[1])
    return pl.pallas_call(
        functools.partial(forward_kernel, groups, first, last),
        out_shape=[pltpu.VMEM((blocks // ROW_PARTS, *shape[1:]), bf16)] * ROW_PARTS if last else [pltpu.VMEM(shape, f32)],
        in_specs=[SMEM, SMEM, HBM] + [VMEM] * (len(groups) + (not first)),
        out_specs=[VMEM] * (ROW_PARTS if last else 1),
        scratch_shapes=[
            pltpu.VMEM((blocks + 1, *shape[1:]), f32),
            pltpu.VMEM((ring, side, side), bf16),
            pltpu.SemaphoreType.DMA((ring,)),
        ],
        cost_estimate=pl.CostEstimate(
            flops=len(groups) * 30 * 2**22, bytes_accessed=len(groups) * 30 * 2**15, transcendentals=0
        ),
        compiler_params=pltpu.CompilerParams(vmem_limit_bytes=16 * 2**20),
        name="forward_group",
    )(plan, spans, tiles, *near(*windows, *([] if first else [total])))


def backward_kernel(groups, plan, spans, tiles, *refs):
    outs = refs[ROW_PARTS:-4]
    grad, total, buffer, sems = refs[-4:]
    blocks = grad.shape[0]
    share = blocks // ROW_PARTS
    for p in range(ROW_PARTS):
        grad[p * share : (p + 1) * share] = refs[p][...]
    span = blocks // PARTS
    total[...] = jnp.zeros_like(total)

    def use(i, packed, tile):
        values = []
        for p, t in zip(packed, tile):
            row = (p >> col_bits) & ((1 << row_bits) - 1)
            values.append(jnp.dot(grad[jnp.minimum(row, blocks - 1)], t[...], preferred_element_type=f32))
        for p, value in zip(packed, values):
            row = (p >> col_bits) & ((1 << row_bits) - 1)
            col = i * span + (p & ((1 << col_bits) - 1))
            total[jnp.where(row == blocks, total.shape[0] - 1, col)] += value

    each_slot(plan, spans, tiles, buffer, sems, groups, use)
    for o, out in enumerate(outs):
        out[...] = total[o * span : (o + 1) * span].astype(out.dtype)


def backward_group(groups, plan, spans, tiles, grads, dtypes):
    blocks, width, side = grads[0].shape
    blocks = blocks * ROW_PARTS
    shape = (blocks, width, side)
    part = (blocks // PARTS, width, side)
    return pl.pallas_call(
        functools.partial(backward_kernel, groups),
        out_shape=[pltpu.VMEM(part, d) for d in dtypes],
        in_specs=[SMEM, SMEM, HBM] + [VMEM] * ROW_PARTS,
        out_specs=[VMEM] * len(dtypes),
        scratch_shapes=[
            pltpu.VMEM(shape, bf16),
            pltpu.VMEM((len(dtypes) * part[0] + 1, width, side), f32),
            pltpu.VMEM((ring, side, side), bf16),
            pltpu.SemaphoreType.DMA((ring,)),
        ],
        cost_estimate=pl.CostEstimate(
            flops=len(groups) * 30 * 2**22, bytes_accessed=len(groups) * 30 * 2**15, transcendentals=0
        ),
        compiler_params=pltpu.CompilerParams(vmem_limit_bytes=16 * 2**20),
        name="backward_group",
    )(plan, spans, tiles, *near(*grads))


def swap(value, first):
    count = lax.axis_size("vertex")
    pairs = []
    for low in range(first, count + first, 2):
        pairs += [(low % count, (low + 1) % count), ((low + 1) % count, low % count)]
    return lax.ppermute(value, "vertex", pairs)


def exchange(value, step):
    count = lax.axis_size("feat")
    return lax.ppermute(value, "feat", [(source, source ^ step) for source in range(count)])


def gather_feat(value):
    far = exchange(value, 2)
    return [value, exchange(value, 1), far, exchange(far, 1)]


def gather_kernel(part, perm, source, out, wide, moved):
    rows = out.shape[0]
    wide[...] = source[...].astype(f32)

    @pl.loop(0, rows // 16)
    def _(step):
        at = step * 16
        for j in range(16):
            moved[pl.ds(at + j, 1), :] = wide[pl.ds(perm[part * rows + at + j], 1), :]

    out[...] = moved[...].astype(out.dtype)


def gather_rows(part, perm, source):
    shape = (perm.shape[0] // PARTS, source.shape[1])
    return pl.pallas_call(
        functools.partial(gather_kernel, part),
        out_shape=pltpu.VMEM(shape, source.dtype),
        in_specs=[SMEM, VMEM],
        out_specs=VMEM,
        scratch_shapes=[pltpu.VMEM(source.shape, f32), pltpu.VMEM(shape, f32)],
        cost_estimate=pl.CostEstimate(flops=0, bytes_accessed=12 * 2**20, transcendentals=0),
        compiler_params=pltpu.CompilerParams(vmem_limit_bytes=8 * 2**20),
        name="gather_rows",
    )(perm, source)


def mix_kernel(part, block_rows, shard, *refs):
    agg, cot, weight = refs[0:4], refs[4:8], refs[8:12]
    act, grad_agg, grad_weight, full, total = refs[-5:]
    rows, width = agg[1].shape
    columns = [pl.ds(pl.multiple_of((shard[0] ^ k) * width, width), width) for k in range(4)]
    for i in range(4):
        for k, c in enumerate(columns):
            full[i * width : (i + 1) * width, k * width : (k + 1) * width] = weight[i][:, c]
    total[...] = jnp.zeros_like(total)
    side = grad_agg.shape[2]

    @pl.loop(0, rows // block_rows)
    def _(step):
        here = pl.ds(pl.multiple_of(step * block_rows, block_rows), block_rows)
        whole = pl.ds(pl.multiple_of(part * rows + step * block_rows, block_rows), block_rows)
        mine = agg[0][here, :]
        mixed = jnp.dot(
            jnp.concatenate([a[here, :] for a in agg], axis=1), full[...], preferred_element_type=f32
        )
        sig = 0.5 + 0.5 * jnp.tanh(0.5 * mixed)
        cotangent = jnp.concatenate([c[whole, :] for c in cot], axis=1).astype(f32)
        grad = (cotangent * sig * (1.0 + mixed * (1.0 - sig))).astype(bf16)
        act[here, :] = (mixed[:, :width] * sig[:, :width]).astype(bf16)
        back = lax.dot_general(full[:width, :], grad, (((1,), (1,)), ((), ())), preferred_element_type=f32)
        for b in range(block_rows // side):
            grad_agg[step * (block_rows // side) + b] = back[:, b * side : (b + 1) * side].astype(bf16)
        total[...] += lax.dot_general(mine, grad, (((0,), (0,)), ((), ())), preferred_element_type=f32)

    for k in range(4):
        grad_weight[shard[0] ^ k] = total[:, k * width : (k + 1) * width]


def mix(part, shard, agg, cot, weight, side, block_rows):
    rows, width = agg[1].shape
    full = weight[0].shape[1]
    return pl.pallas_call(
        functools.partial(mix_kernel, part, block_rows),
        out_shape=[
            jax.ShapeDtypeStruct((rows, width), bf16),
            pltpu.VMEM((rows // side, width, side), bf16),
            pltpu.VMEM((full // width, width, width), f32),
        ],
        in_specs=[SMEM] + [VMEM] * 12,
        out_specs=[VMEM] * 3,
        scratch_shapes=[pltpu.VMEM((full, full), bf16), pltpu.VMEM((width, full), f32)],
        cost_estimate=pl.CostEstimate(
            flops=3 * rows * full * full, bytes_accessed=8 * rows * full, transcendentals=rows * full
        ),
        compiler_params=pltpu.CompilerParams(vmem_limit_bytes=16 * 2**20),
        name="mix",
    )(shard, *near(*agg, *cot), *weight)


def add_kernel(carried, own, out):
    out[...] = (carried[...].astype(f32) + own[...].astype(f32)).astype(bf16)


def add_part(carried, own):
    return pl.pallas_call(
        add_kernel,
        out_shape=pltpu.VMEM(carried.shape, bf16),
        in_specs=[VMEM] * 2,
        out_specs=VMEM,
        cost_estimate=pl.CostEstimate(flops=0, bytes_accessed=6 * carried.size, transcendentals=0),
        compiler_params=pltpu.CompilerParams(vmem_limit_bytes=4 * 2**20),
        name="add_part",
    )(*near(carried, own))


def scatter_kernel(perm, own, left, right, out, moved, wide):
    blocks, width, side = own.shape

    @pl.loop(0, blocks // together)
    def _(step):
        for k in range(together):
            b = step * together + k
            wide[k] = (own[b] + left[b].astype(f32) + right[b].astype(f32)).T
        for k in range(together):
            at = (step * together + k) * side
            for j in range(side):
                moved[pl.ds(perm[at + j], 1), :] = wide[k, j : j + 1, :]

    out[...] = moved[...].astype(out.dtype)


def scatter_rows(perm, own, left, right):
    width = own.shape[1]
    rows = perm.shape[0]
    return pl.pallas_call(
        scatter_kernel,
        out_shape=jax.ShapeDtypeStruct((rows, width), bf16),
        in_specs=[SMEM] + [VMEM] * 3,
        out_specs=VMEM,
        scratch_shapes=[pltpu.VMEM((rows, width), f32), pltpu.VMEM((together, own.shape[2], width), f32)],
        cost_estimate=pl.CostEstimate(flops=0, bytes_accessed=12 * 2**20, transcendentals=0),
        compiler_params=pltpu.CompilerParams(vmem_limit_bytes=8 * 2**20),
        name="scatter_rows",
    )(perm, *near(own, left, right))


def sum_share(value):
    split = value.reshape(lax.axis_size("vertex"), -1, value.shape[-1])
    return jnp.sum(lax.all_to_all(split, "vertex", 0, 0, tiled=True), axis=0)


def spread_shares(mine, scale):
    spread = jnp.broadcast_to((mine * scale)[None], (lax.axis_size("vertex"), *mine.shape))
    return lax.all_to_all(spread, "vertex", 0, 0, tiled=True)


def body(features, tiles, tile_row, tile_col, permutation, weight, cotangent):
    rows, width = features.shape
    side = tiles.shape[1]
    blocks = rows // side
    devices = lax.axis_size("vertex")
    here = lax.axis_index("vertex")
    local = permutation - here * rows
    shard = lax.axis_index("feat").astype(jnp.int32).reshape(1)
    span = rows // ROW_PARTS
    scale = 1.0 / math.sqrt(rows * devices)
    tiles = pltpu.with_memory_space_constraint(tiles, pltpu.HBM)

    far = exchange(cotangent, 2)
    weight_far = exchange(weight, 2)
    ordered = gather_rows(0, local, features)
    plan, spans = slot_plan(tile_row, tile_col, here, blocks, devices)
    ordered, far, weight_far = lax.optimization_barrier((ordered, far, weight_far))

    even, odd = swap(ordered, 0), swap(ordered, 1)
    windows = [ordered, even, odd]
    weight_full = [weight, exchange(weight, 1), weight_far, exchange(weight_far, 1)]
    cot_full = [cotangent, exchange(cotangent, 1), far, exchange(far, 1)]
    for reach in range(2, REACH + 1):
        even, odd, plan = lax.optimization_barrier((even, odd, plan))
        even, odd = swap(odd, 0), swap(even, 1)
        windows += [even, odd]
    (total,) = forward_group(keys(*range(REACH)), True, False, plan, spans, tiles, windows[:-2], None)
    total, weight_full, cot_full = lax.optimization_barrier((total, weight_full, cot_full))
    total = forward_group(keys(REACH), False, True, plan, spans, tiles, windows[-2:], total)
    aggregated = [t.reshape(span, width) for t in total]

    acts, grads, terms = [], [], []
    for p in range(ROW_PARTS):
        act, grad, term = mix(p, shard, gather_feat(aggregated[p]), cot_full, weight_full, side, 6 * side)
        acts.append(act)
        grads.append(grad)
        terms.append(term)
    activations = jnp.concatenate(acts, axis=0)

    def after(token, value):
        return lax.optimization_barrier((exchange(token[0, :16], 1), value))[1]

    even, odd = backward_group(keys(REACH), plan, spans, tiles, grads, [bf16] * 2)
    share = sum_share(after(even, sum(terms)))
    even, odd = swap(even, 0), swap(odd, 1)
    own = backward_group(keys(2), plan, spans, tiles, grads, [bf16] * 2)
    even, odd, plan = lax.optimization_barrier((even, odd, plan))
    even, odd = add_part(odd, own[0]), add_part(even, own[1])
    even, odd = swap(even, 0), swap(odd, 1)
    own = backward_group(keys(0, 1), plan, spans, tiles, grads, [f32] + [bf16] * 2)
    even, odd = add_part(odd, own[1]), add_part(even, own[2])
    share = spread_shares(after(even, share), scale)
    even, odd = swap(even, 0), swap(odd, 1)
    even, odd, activations = lax.optimization_barrier((even, odd, activations))
    grad_features = scatter_rows(local, own[0], even, odd)
    share = share.reshape(-1, width, width)
    grad_weight = jnp.concatenate([share[k] for k in range(share.shape[0])], axis=1)
    return (activations, grad_features, grad_weight)


def solution(mesh):
    in_specs = (
        P("vertex", "feat"),
        P("vertex", None, None),
        P("vertex"),
        P("vertex"),
        P("vertex"),
        P("feat", None),
        P("vertex", "feat"),
    )
    out_specs = (P("vertex", "feat"), P("vertex", "feat"), P("feat", None))
    return jax.shard_map(body, mesh=mesh, in_specs=in_specs, out_specs=out_specs, check_vma=False)
```
